256 devices in a mesh: group: 4 (over y), shard: 64 (over x, z, core).
Axes of the slice: x: 4, y: 4, z: 8, core: 2. Of those that a mesh axis runs over, the one named last changes fastest.
Arguments:
- activations: bfloat16 [4, 128, 256, 1024], P('group', 'shard'), may hold values from -7 to 7
- out_grad: bfloat16 [4, 128, 256, 1024], P('group', None, 'shard'), may hold values from -1.5 to 1.5
- embedding: bfloat16 [512, 1024], replicated, may hold values from -6 to 6
- counts: int32 [4, 8], P('group'), may hold values from 0 to 256, as said below
- offsets: int32 [4, 8], P('group'), may hold values from 0 to 8, as said below
- layout: int32 [4, 256], P('group'), may hold values from 0 to 511
Outputs:
- input_grad: bfloat16 [4, 128, 256, 1024], P('group', 'shard')
- embedding_grad: float32 [512, 1024], P('group')
The draws below stay inside these ranges and needn't reach their ends.
Inputs may be any that keep to these rules, and one draw needn't show every extreme that they name: `counts`: A used session slot holds 19 to 256 electrodes; slots after the used ones hold 0. `offsets`: used session slots come first; the first starts at block 0 and each next one where the previous ends, a session taking ceil(count / 32) blocks, all sessions together exactly 8 blocks; unused slots hold 8.
All inputs are finite; a program needn't handle non-finite values.
Results may differ from the reference program's by a relative error of at most 0.012.
The reference program's roundings to bfloat16 on the way (of `embedded`, `weights`, `mixed`, `grad_scores` and `mixed_grad`) count: a program that leaves them out, or rounds other values in their place, can miss the bound.
Values may be sent and summed in bfloat16 or wider, within the bound.
A program may use at most 64 MiB of HBM per device.

```python
import math
import jax
import jax.numpy as jnp
from jax import lax

D = 1024
HEADS = 16
TEMPLATES = 512
PATCHES = 128
BLOCK = 32
MIN_ELEC = 19
SESS_BLOCKS = 8
NE = 256
N_GROUP = 4


def session_table(key):
    key_cut = jax.random.fold_in(key, 11)
    key_short = jax.random.fold_in(key, 12)
    blocks = NE // BLOCK
    position = jnp.arange(blocks, dtype=jnp.int32)
    boundary = (position % SESS_BLOCKS == 0).astype(jnp.int32)
    starts = jax.random.randint(key_cut, (N_GROUP, blocks), 0, 2, dtype=jnp.int32)
    starts = jnp.maximum(starts, boundary[None, :])
    first_group = (jnp.arange(N_GROUP, dtype=jnp.int32) == 0)[:, None]
    starts = jnp.where(first_group, boundary[None, :], starts)
    owner_index = jnp.cumsum(starts, axis=1) - 1
    member = owner_index[:, :, None] == position[None, None, :]
    offsets = jnp.min(jnp.where(member, position[None, :, None], blocks), axis=1)
    span_blocks = jnp.sum(member.astype(jnp.int32), axis=1)
    shortfall = jax.random.randint(key_short, (N_GROUP, blocks), 0, BLOCK, dtype=jnp.int32)
    shortfall = jnp.where(first_group & (position[None, :] == 0), 0, shortfall)
    counts = jnp.maximum(span_blocks * BLOCK - shortfall, MIN_ELEC)
    counts = jnp.where(span_blocks > 0, counts, 0)
    return (counts.astype(jnp.int32), offsets.astype(jnp.int32))


def draw_counts(key, part):
    return session_table(key)[0]


def draw_offsets(key, part):
    return session_table(key)[1]


def draw_activations(key, part):
    key_value = jax.random.fold_in(key, 21)
    shape = (N_GROUP, PATCHES, NE, D)
    values = jnp.clip(jax.random.normal(key_value, shape, jnp.float32), -6.0, 6.0)
    return values.astype(jnp.bfloat16)


def with_ends(drawn, stream_key, low, high):
    extent = drawn.shape
    index_at = [jax.random.randint(jax.random.fold_in(stream_key, axis), (), 0, extent[axis]) for axis in range(len(extent))]
    drawn = drawn.at[tuple(index_at)].set(low)
    longest = extent.index(max(extent))
    index_at[longest] = (index_at[longest] + 1) % extent[longest]
    return drawn.at[tuple(index_at)].set(high)


def block_levels(rng, dims, pieces, least, largest):
    loudness, own = 1.0, jax.random.fold_in(rng, 6)
    for dim, parts in pieces:
        heights = jnp.exp(jax.random.uniform(jax.random.fold_in(own, dim), (parts,), jnp.float32, least / len(pieces), largest / len(pieces)))
        loudness = loudness * jnp.repeat(heights, dims[dim] // parts).reshape([-1 if axis == dim else 1 for axis in range(len(dims))])
    return loudness


def scatter_about(key, shape, scale, bound, split=(), kind=jnp.bfloat16):
    values = scale * jax.random.normal(key, shape, jnp.float32)
    if split:
        values = values * block_levels(key, shape, split, -0.22, 0.18)
    return jnp.clip(values, -bound, bound).astype(kind)


def setup_inputs(seed: int = 0) -> dict:
    splits = jax.random.split(jax.random.key(seed), 7)
    return {
        "activations": draw_activations(jax.random.fold_in(splits[6], 71), 0),
        "out_grad": scatter_about(splits[1], (N_GROUP, PATCHES, NE, D), 0.25, 1.5, ((0, 4), (2, 64))),
        "embedding": scatter_about(splits[2], (TEMPLATES, D), 1.0, 6.0),
        "counts": draw_counts(jax.random.fold_in(splits[6], 71), 0),
        "offsets": draw_offsets(jax.random.fold_in(splits[6], 71), 0),
        "layout": with_ends(jax.random.randint(splits[5], (N_GROUP, NE), 0, TEMPLATES), jax.random.fold_in(splits[5], 1), 0, TEMPLATES - 1).astype(jnp.int32),
    }


def product(form, left, right):
    return jnp.einsum(form, left.astype(jnp.float32), right.astype(jnp.float32), precision=lax.Precision.HIGHEST)

def attend(values, allowed):
    length = values.shape[0]
    head_split = values.reshape(length, HEADS, -1)
    score_scale = 0.5 / math.sqrt(head_split.shape[-1])
    scores = product('qhd,khd->hqk', head_split, head_split) * score_scale
    scores = jnp.where(allowed[None], scores, -1e+30)
    row_max = lax.optimization_barrier(jnp.max(scores, axis=-1, keepdims=True))
    exponent = jnp.exp(scores - row_max)
    weights = (exponent / lax.optimization_barrier(jnp.sum(exponent, axis=-1, keepdims=True))).astype(jnp.bfloat16)
    attended = product('hqk,khd->qhd', weights, head_split)
    return (head_split, weights, attended)

def attend_back(values, allowed, cotangent):
    head_split, weights, attended = attend(values, allowed)
    length = values.shape[0]
    score_scale = 0.5 / math.sqrt(head_split.shape[-1])
    grad_heads = cotangent.reshape(length, HEADS, -1)
    row_delta = lax.optimization_barrier(jnp.sum(grad_heads.astype(jnp.float32) * attended, axis=-1))
    grad_weights = product('qhd,khd->hqk', grad_heads, head_split)
    grad_scores = (weights.astype(jnp.float32) * (grad_weights - jnp.transpose(row_delta)[:, :, None])).astype(jnp.bfloat16)
    grad_values = score_scale * (product('hqk,khd->qhd', grad_scores, head_split) + product('hqk,qhd->khd', grad_scores, head_split))
    grad_values = grad_values + product('hqk,qhd->khd', weights, grad_heads)
    return grad_values.reshape(length, -1)

def session_pairs(counts, offsets, electrodes):
    slot_index = jnp.arange(electrodes, dtype=jnp.int32)
    block_index = slot_index // BLOCK
    member = (offsets[None, :] <= block_index[:, None]).astype(jnp.int32)
    session = lax.optimization_barrier(jnp.sum(member, axis=1)) - 1
    chosen = (jnp.arange(offsets.shape[0], dtype=jnp.int32)[None, :] == session[:, None]).astype(jnp.int32)
    first_slot = lax.optimization_barrier(jnp.sum(chosen * offsets[None, :], axis=1)) * BLOCK
    live_count = lax.optimization_barrier(jnp.sum(chosen * counts[None, :], axis=1))
    is_live = slot_index - first_slot < live_count
    return (session[:, None] == session[None, :]) & is_live[None, :]

def reference(activations, out_grad, embedding, counts, offsets, layout):
    input_rows = []
    tables = jnp.zeros((TEMPLATES, D), jnp.float32)
    full_mask = jnp.ones((PATCHES, PATCHES), dtype=bool)
    for group_index in range(N_GROUP):
        allowed = session_pairs(counts[group_index], offsets[group_index], NE)
        onehot = (layout[group_index][:, None] == jnp.arange(TEMPLATES, dtype=jnp.int32)[None, :]).astype(jnp.float32)
        layout_rows = jnp.dot(onehot, embedding.astype(jnp.float32), precision=lax.Precision.HIGHEST)
        embedded = (activations[group_index].astype(jnp.float32) + layout_rows[None]).astype(jnp.bfloat16)

        def spatial(values):
            return (values.astype(jnp.float32) + attend(values, allowed)[2].reshape(NE, D)).astype(jnp.bfloat16)
        mixed = lax.map(spatial, embedded)

        def temporal(couple):
            values, cotangent = couple
            return (cotangent.astype(jnp.float32) + attend_back(values, full_mask, cotangent)).astype(jnp.bfloat16)
        mixed_grad = lax.map(temporal, (jnp.moveaxis(mixed, 1, 0), jnp.moveaxis(out_grad[group_index], 1, 0)))
        mixed_grad = jnp.moveaxis(mixed_grad, 0, 1)

        def spatial_back(couple):
            values, cotangent = couple
            return cotangent.astype(jnp.float32) + attend_back(values, allowed, cotangent)
        full_grad = lax.map(spatial_back, (embedded, mixed_grad))
        input_rows.append(full_grad.astype(jnp.bfloat16))
        electrode_grad = lax.optimization_barrier(jnp.sum(full_grad, axis=0))
        tables = tables + jnp.dot(jnp.transpose(onehot), electrode_grad, precision=lax.Precision.HIGHEST)
    return (jnp.stack(input_rows), tables)
```

```python
import math

import jax
import jax.numpy as jnp
from jax import lax
from jax.sharding import PartitionSpec as P

HEADS = 16
BLOCK = 32


def product(form, left, right):
    return jnp.einsum(form, left, right, preferred_element_type=jnp.float32)


def attend(values, allowed):
    length = values.shape[0]
    head_split = values.reshape(length, HEADS, -1)
    score_scale = 0.5 / math.sqrt(head_split.shape[-1])
    scores = product("qhd,khd->hqk", head_split, head_split) * score_scale
    scores = jnp.where(allowed[None], scores, -1e30)
    row_max = jnp.max(scores, axis=-1, keepdims=True)
    exponent = jnp.exp(scores - row_max)
    weights = (exponent / jnp.sum(exponent, axis=-1, keepdims=True)).astype(jnp.bfloat16)
    attended = product("hqk,khd->qhd", weights, head_split)
    return (head_split, weights, attended)


def attend_back(values, allowed, cotangent):
    head_split, weights, attended = attend(values, allowed)
    length = values.shape[0]
    score_scale = 0.5 / math.sqrt(head_split.shape[-1])
    grad_heads = cotangent.reshape(length, HEADS, -1)
    row_delta = jnp.sum(grad_heads.astype(jnp.float32) * attended, axis=-1)
    grad_weights = product("qhd,khd->hqk", grad_heads, head_split)
    grad_scores = (
        weights.astype(jnp.float32) * (grad_weights - jnp.transpose(row_delta)[:, :, None])
    ).astype(jnp.bfloat16)
    grad_values = score_scale * (
        product("hqk,khd->qhd", grad_scores, head_split)
        + product("hqk,qhd->khd", grad_scores, head_split)
    )
    grad_values = grad_values + product("hqk,qhd->khd", weights, grad_heads)
    return grad_values.reshape(length, -1)


def session_pairs(counts, offsets, electrodes):
    slot_index = jnp.arange(electrodes, dtype=jnp.int32)
    block_index = slot_index // BLOCK
    member = (offsets[None, :] <= block_index[:, None]).astype(jnp.int32)
    session = jnp.sum(member, axis=1) - 1
    chosen = (jnp.arange(offsets.shape[0], dtype=jnp.int32)[None, :] == session[:, None]).astype(
        jnp.int32
    )
    first_slot = jnp.sum(chosen * offsets[None, :], axis=1) * BLOCK
    live_count = jnp.sum(chosen * counts[None, :], axis=1)
    is_live = slot_index - first_slot < live_count
    return (session[:, None] == session[None, :]) & is_live[None, :]


def body(activations, out_grad, embedding, counts, offsets, layout):
    local_in = activations[0]
    electrodes = local_in.shape[1]
    templates = embedding.shape[0]
    allowed = session_pairs(counts[0], offsets[0], electrodes)
    onehot = (layout[0][:, None] == jnp.arange(templates, dtype=jnp.int32)[None, :]).astype(
        jnp.bfloat16
    )
    layout_rows = jnp.dot(onehot, embedding, preferred_element_type=jnp.float32)
    embedded = (local_in.astype(jnp.float32) + layout_rows[None]).astype(jnp.bfloat16)

    def spatial(values):
        return (
            values.astype(jnp.float32) + attend(values, allowed)[2].reshape(electrodes, -1)
        ).astype(jnp.bfloat16)

    mixed = lax.map(spatial, embedded)
    gathered = lax.all_to_all(mixed[None], "shard", split_axis=2, concat_axis=1, tiled=True)
    patches = gathered.shape[1]
    full_mask = jnp.ones((patches, patches), dtype=bool)

    def temporal(couple):
        values, cotangent = couple
        return (cotangent.astype(jnp.float32) + attend_back(values, full_mask, cotangent)).astype(
            jnp.bfloat16
        )

    mixed_grad = lax.map(
        temporal, (jnp.moveaxis(gathered[0], 1, 0), jnp.moveaxis(out_grad[0], 1, 0))
    )
    returned = lax.all_to_all(
        jnp.moveaxis(mixed_grad, 0, 1)[None], "shard", split_axis=1, concat_axis=2, tiled=True
    )

    def spatial_back(couple):
        values, cotangent = couple
        return cotangent.astype(jnp.float32) + attend_back(values, allowed, cotangent)

    full_grad = lax.map(spatial_back, (embedded, returned[0]))
    input_grad = full_grad.astype(jnp.bfloat16)[None]
    electrode_grad = jnp.sum(full_grad, axis=0)
    shards = lax.axis_size("shard")
    groups = lax.axis_size("group")
    width = local_in.shape[2]
    pieces = jnp.transpose(electrode_grad).astype(jnp.bfloat16)
    pieces = pieces.reshape(shards, width // shards, electrodes)
    arrived = lax.all_to_all(pieces, "shard", split_axis=0, concat_axis=0, tiled=True)
    own_columns = jnp.sum(arrived.astype(jnp.float32), axis=0)
    column_table = jnp.dot(
        own_columns.astype(jnp.bfloat16), onehot, preferred_element_type=jnp.float32
    )
    own_rows = templates // groups
    column_table = column_table.reshape(width // shards, groups, own_rows)
    from_groups = lax.all_to_all(
        jnp.moveaxis(column_table, 1, 0), "group", split_axis=0, concat_axis=0, tiled=True
    )
    own_part = jnp.sum(from_groups, axis=0)
    gathered_table = lax.all_gather(own_part, "shard", axis=0, tiled=True)
    table_grad = jnp.transpose(gathered_table)
    return (input_grad, table_grad)


def solution(mesh):
    placed = (
        P("group", "shard", None, None),
        P("group", None, "shard", None),
        P(),
        P("group", None),
        P("group", None),
        P("group", None),
    )
    return jax.shard_map(
        body,
        mesh=mesh,
        in_specs=placed,
        out_specs=(P("group", "shard", None, None), P("group", None)),
        check_vma=False,
    )
```

```python
import functools

import jax
import jax.numpy as jnp
from jax import lax
from jax.experimental import pallas as pl
from jax.experimental.pallas import tpu as pltpu
from jax.sharding import PartitionSpec as P

MESH = pl.DeviceIdType.MESH
SHARDS = 64
GROUPS = 4
HALF = 64
LANES = 128
PAIRS = 8
CHUNKS = 4
PER_CHUNK = PAIRS // CHUNKS
SLOTS = 256
PATCHES = 128
TEMPLATES = 512
WIDTH = 1024
OWN_COLS = WIDTH // SHARDS
OWN_ROWS = TEMPLATES // GROUPS
SCALE = 0.0625
BLOCK_SHIFT = 5
SESSIONS = 8
F32 = jnp.float32
BF16 = jnp.bfloat16


def mm(a, b):
    return lax.dot_general(a, b, (((1,), (0,)), ((), ())), preferred_element_type=F32)


def mm_nt(a, b):
    return lax.dot_general(a, b, (((1,), (1,)), ((), ())), preferred_element_type=F32)


def head_masks(values):
    lane = lax.broadcasted_iota(jnp.int32, values.shape, 1)
    zero = jnp.zeros_like(values)
    return jnp.where(lane < HALF, values, zero), jnp.where(lane < HALF, zero, values)


def column_softmax(scores):
    top = jnp.max(scores, axis=0, keepdims=True)
    exponent = jnp.exp(scores - top)
    total = jnp.sum(exponent, axis=0, keepdims=True)
    return (exponent * (1.0 / total)).astype(BF16)


def turned_grad_scores(weights_t, grad_weights_t):
    wide = weights_t.astype(F32)
    row_delta = jnp.sum(wide * grad_weights_t, axis=0, keepdims=True)
    return (wide * (grad_weights_t - row_delta)).astype(BF16)


def spatial_pair(values, bias):
    scaled = values * jnp.asarray(SCALE, BF16)
    values_t = jnp.transpose(values)
    weights, parts = [], []
    for head, masked in enumerate(head_masks(values)):
        scores_t = mm_nt(scaled, masked) + bias
        weights_t = column_softmax(scores_t)
        weights.append(weights_t)
        parts.append(mm(values_t[head * HALF : (head + 1) * HALF], weights_t))
    attended = jnp.transpose(jnp.concatenate(parts, axis=0))
    return values.astype(F32) + attended, weights


def temporal_pair(values, cotangent):
    scaled = values * jnp.asarray(SCALE, BF16)
    scaled_t = jnp.transpose(scaled)
    stacked = jnp.concatenate(head_masks(values), axis=0)
    stacked_grad = jnp.concatenate(head_masks(cotangent), axis=0)
    scores_t = mm_nt(scaled, stacked)
    weights_t = column_softmax(scores_t)
    grad_weights_t = mm_nt(values, stacked_grad)
    grad_scores_t = turned_grad_scores(weights_t, grad_weights_t)
    stacked_scaled = stacked * jnp.asarray(SCALE, BF16)
    direct = mm(grad_scores_t, stacked_scaled) + mm(weights_t, stacked_grad)
    turned = mm(scaled_t, grad_scores_t)
    row = lax.broadcasted_iota(jnp.int32, (LANES, LANES), 0)
    turned = jnp.where(row < HALF, turned[:, :LANES], turned[:, LANES:])
    return cotangent.astype(F32) + direct + jnp.transpose(turned)


def spatial_back_pair(values, weights, cotangent):
    scaled = values * jnp.asarray(SCALE, BF16)
    scaled_t = jnp.transpose(scaled)
    total = cotangent.astype(F32)
    parts = []
    pieces = zip(weights, head_masks(scaled), head_masks(cotangent))
    for head, (weights_t, scaled_head, grad_head) in enumerate(pieces):
        grad_weights_t = mm_nt(values, grad_head)
        grad_scores_t = turned_grad_scores(weights_t, grad_weights_t)
        total = total + (mm(grad_scores_t, scaled_head) + mm(weights_t, grad_head))
        parts.append(mm(scaled_t[head * HALF : (head + 1) * HALF], grad_scores_t))
    return total + jnp.transpose(jnp.concatenate(parts, axis=0))


def weave(first, second, roll):
    columns = first.shape[1]
    first = first.reshape(SLOTS // 8, 8, columns)
    second = second.reshape(SLOTS // 8, 8, columns)
    low = lax.broadcasted_iota(jnp.int32, first.shape, 1) < 4
    even = jnp.where(low, first, roll(second, 4, 1))
    odd = jnp.where(low, roll(first, 4, 1), second)
    return jnp.stack([even, odd], axis=1).reshape(SHARDS, 8, columns)


def unweave(blocks, roll):
    columns = blocks.shape[2]
    blocks = blocks.reshape(SLOTS // 8, 2, 8, columns)
    even, odd = blocks[:, 0], blocks[:, 1]
    low = lax.broadcasted_iota(jnp.int32, even.shape, 1) < 4
    first = jnp.where(low, even, roll(odd, 4, 1))
    second = jnp.where(low, roll(even, 4, 1), odd)
    return first.reshape(SLOTS, columns), second.reshape(SLOTS, columns)


def session_bias(counts, offsets):
    def place(slot):
        block = lax.shift_right_logical(slot, BLOCK_SHIFT)
        start = jnp.zeros_like(slot)
        count = jnp.zeros_like(slot)
        for j in range(SESSIONS):
            reached = block >= offsets[0, j]
            start = jnp.where(reached, offsets[0, j], start)
            count = jnp.where(reached, counts[0, j], count)
        return start, count

    keys = lax.broadcasted_iota(jnp.int32, (SLOTS, LANES), 0)
    key_start, key_count = place(keys)
    live = keys - (1 << BLOCK_SHIFT) * key_start < key_count
    key_start = jnp.where(live, key_start, -1)
    halves = []
    for half in range(SLOTS // LANES):
        queries = lax.broadcasted_iota(jnp.int32, (SLOTS, LANES), 1) + half * LANES
        query_start, _ = place(queries)
        halves.append(jnp.where(query_start == key_start, 0.0, -1e30))
    return jnp.concatenate(halves, axis=1)


def kernel(
    counts,
    offsets,
    act,
    out_grad,
    table,
    layout,
    input_grad,
    table_grad,
    embedded,
    saved,
    bias,
    chosen,
    chosen_t,
    rows_in,
    rows_grad,
    rows_out,
    send_mix,
    recv_mix,
    send_back,
    recv_back,
    send_sum,
    recv_sum,
    send_group,
    recv_group,
    send_part,
    recv_part,
    mix_sems,
    back_sems,
    sum_sems,
    group_sems,
    part_sems,
):
    me = lax.axis_index("shard")
    group = lax.axis_index("group")

    barrier = pltpu.get_barrier_semaphore()

    @pl.loop(1, SHARDS)
    def _(step):
        peer = lax.rem(me + step, SHARDS)
        pl.semaphore_signal(barrier, inc=1, device_id=(group, peer), device_id_type=MESH)

    for step in range(1, GROUPS):
        other = lax.rem(group + step, GROUPS)
        pl.semaphore_signal(barrier, inc=1, device_id=(other, me), device_id_type=MESH)

    bias[...] = session_bias(counts, offsets)
    template = lax.broadcasted_iota(jnp.int32, (TEMPLATES, SLOTS), 0)
    hit = jnp.where(template == layout[...], 1.0, 0.0)
    chosen_t[...] = hit.astype(BF16)
    chosen[...] = jnp.transpose(hit).astype(BF16)

    def block_copy(source, target, sems, chunk, peer, slot):
        pairs = pl.ds(chunk * PER_CHUNK, PER_CHUNK)
        return pltpu.make_async_remote_copy(
            src_ref=source.at[pairs, peer],
            dst_ref=target.at[pairs, slot],
            send_sem=sems.at[0, chunk],
            recv_sem=sems.at[1, chunk],
            device_id=(group, peer),
            device_id_type=MESH,
        )

    def all_blocks(source, target, sems, chunk):
        pairs = pl.ds(chunk * PER_CHUNK, PER_CHUNK)
        others = pl.ds(0, SHARDS - 1)
        return pltpu.make_async_remote_copy(
            src_ref=source.at[pairs, others],
            dst_ref=target.at[pairs, others],
            send_sem=sems.at[0, chunk],
            recv_sem=sems.at[1, chunk],
            device_id=(group, lax.rem(me + 1, SHARDS)),
            device_id_type=MESH,
        )

    def send_chunk(source, target, sems, chunk):
        @pl.loop(1, SHARDS)
        def _(step):
            peer = lax.rem(me + step, SHARDS)
            block_copy(source, target, sems, chunk, peer, me).start()

        for pair in range(PER_CHUNK):
            at = chunk * PER_CHUNK + pair
            target[at, me] = source[at, me]

    def spatial_step(pair):
        lanes = pl.ds(pl.multiple_of(pair * LANES, LANES), LANES)
        rows = mm(chosen[...], table[:, lanes])
        mixed = []
        for patch in range(2):
            values = (act[0, patch, :, lanes].astype(F32) + rows).astype(BF16)
            embedded[patch, pair] = values
            out, weights = spatial_pair(values, bias[...])
            for head in range(2):
                saved[patch, pair, head] = weights[head]
            mixed.append(out)
        send_mix[pair] = weave(mixed[0], mixed[1], pltpu.roll).astype(BF16)

    def temporal_step(pair):
        lanes = pl.ds(pl.multiple_of(pair * LANES, LANES), LANES)
        rows_in[...] = recv_mix[pair].astype(F32).reshape(PATCHES * 4, LANES)
        rows_grad[:, 0:4, :] = out_grad[0, :, :, lanes].astype(F32)
        flat_grad = rows_grad.reshape(PATCHES * 8, LANES)
        for slot in range(4):
            values = rows_in[pl.ds(slot, PATCHES, stride=4), :].astype(BF16)
            cotangent = flat_grad[pl.ds(slot, PATCHES, stride=8), :].astype(BF16)
            rows_out[pl.ds(slot, PATCHES, stride=4), :] = temporal_pair(values, cotangent)
        send_back[pair] = rows_out[...].reshape(SHARDS, 8, LANES).astype(BF16)

    def back_step(pair):
        lanes = pl.ds(pl.multiple_of(pair * LANES, LANES), LANES)
        grads = unweave(recv_back[pair].astype(F32), pltpu.roll)
        electrode = None
        for patch in range(2):
            full = spatial_back_pair(
                embedded[patch, pair],
                [saved[patch, pair, head] for head in range(2)],
                grads[patch].astype(BF16),
            )
            input_grad[0, patch, :, lanes] = full.astype(BF16)
            electrode = full if electrode is None else electrode + full
        owners = LANES // OWN_COLS
        send_sum[pl.ds(pair * owners, owners)] = (
            jnp.transpose(electrode).astype(BF16).reshape(owners, OWN_COLS, SLOTS)
        )

    def over_pairs(chunk, step):
        @pl.loop(0, PER_CHUNK)
        def _(pair):
            step(chunk * PER_CHUNK + pair)

    over_pairs(0, spatial_step)
    pl.semaphore_wait(barrier, SHARDS - 1 + GROUPS - 1)
    send_chunk(send_mix, recv_mix, mix_sems, 0)

    @pl.loop(1, CHUNKS)
    def _(chunk):
        over_pairs(chunk, spatial_step)
        send_chunk(send_mix, recv_mix, mix_sems, chunk)

    @pl.loop(0, CHUNKS)
    def _(chunk):
        all_blocks(send_mix, recv_mix, mix_sems, chunk).wait_recv()
        over_pairs(chunk, temporal_step)
        send_chunk(send_back, recv_back, back_sems, chunk)

    @pl.loop(0, CHUNKS)
    def _(chunk):
        all_blocks(send_back, recv_back, back_sems, chunk).wait_recv()
        over_pairs(chunk, back_step)

    def to_shards(source_at, target, sems):
        @pl.loop(1, SHARDS)
        def _(step):
            peer = lax.rem(me + step, SHARDS)
            pltpu.make_async_remote_copy(
                src_ref=source_at(peer),
                dst_ref=target.at[me],
                send_sem=sems.at[0],
                recv_sem=sems.at[1],
                device_id=(group, peer),
                device_id_type=MESH,
            ).start()

    def from_shards(target, sems):
        others = pl.ds(0, SHARDS - 1)
        return pltpu.make_async_remote_copy(
            src_ref=target.at[others],
            dst_ref=target.at[others],
            send_sem=sems.at[0],
            recv_sem=sems.at[1],
            device_id=(group, lax.rem(me + 1, SHARDS)),
            device_id_type=MESH,
        )

    to_shards(lambda peer: send_sum.at[peer], recv_sum, sum_sems)
    recv_sum[me] = send_sum[me]
    from_shards(recv_sum, sum_sems).wait_recv()

    columns = jnp.zeros((OWN_COLS, SLOTS), F32)
    for part in range(8):
        columns = columns + jnp.sum(recv_sum[part * 8 : part * 8 + 8].astype(F32), axis=0)
    high = columns.astype(BF16)
    low = (columns - high.astype(F32)).astype(BF16)
    own = mm_nt(high, chosen_t[...]) + mm_nt(low, chosen_t[...])
    for other in range(GROUPS):
        send_group[other] = own[:, other * OWN_ROWS : (other + 1) * OWN_ROWS]
    copies = []
    for step in range(1, GROUPS):
        other = lax.rem(group + step, GROUPS)
        copy = pltpu.make_async_remote_copy(
            src_ref=send_group.at[other],
            dst_ref=recv_group.at[step],
            send_sem=group_sems.at[0, step],
            recv_sem=group_sems.at[1, step],
            device_id=(other, me),
            device_id_type=MESH,
        )
        copy.start()
        copies.append(copy)
    part = send_group[group]
    for step, copy in enumerate(copies):
        copy.wait_recv()
        part = part + recv_group[step + 1]
    part = part.astype(BF16)
    send_part[...] = part
    to_shards(lambda peer: send_part, recv_part, part_sems)
    recv_part[me] = part
    from_shards(recv_part, part_sems).wait_recv()
    turned = recv_part[...].astype(F32).reshape(WIDTH, OWN_ROWS)
    table_grad[...] = jnp.transpose(turned)

    @pl.loop(0, CHUNKS)
    def _(chunk):
        all_blocks(send_mix, recv_mix, mix_sems, chunk).wait_send()
        all_blocks(send_back, recv_back, back_sems, chunk).wait_send()

    from_shards(recv_sum, sum_sems).wait_send()
    from_shards(recv_part, part_sems).wait_send()
    for copy in copies:
        copy.wait_send()


def body(activations, out_grad, embedding, counts, offsets, layout):
    vmem = pl.BlockSpec(memory_space=pltpu.VMEM)
    smem = pl.BlockSpec(memory_space=pltpu.SMEM)
    scratch = [
        pltpu.VMEM((2, PAIRS, SLOTS, LANES), BF16),
        pltpu.VMEM((2, PAIRS, 2, SLOTS, SLOTS), BF16),
        pltpu.VMEM((SLOTS, SLOTS), F32),
        pltpu.VMEM((SLOTS, TEMPLATES), BF16),
        pltpu.VMEM((TEMPLATES, SLOTS), BF16),
        pltpu.VMEM((PATCHES * 4, LANES), F32),
        pltpu.VMEM((PATCHES, 8, LANES), F32),
        pltpu.VMEM((PATCHES * 4, LANES), F32),
        pltpu.VMEM((PAIRS, SHARDS, 8, LANES), BF16),
        pltpu.VMEM((PAIRS, SHARDS, 8, LANES), BF16),
        pltpu.VMEM((PAIRS, SHARDS, 8, LANES), BF16),
        pltpu.VMEM((PAIRS, SHARDS, 8, LANES), BF16),
        pltpu.VMEM((SHARDS, OWN_COLS, SLOTS), BF16),
        pltpu.VMEM((SHARDS, OWN_COLS, SLOTS), BF16),
        pltpu.VMEM((GROUPS, OWN_COLS, OWN_ROWS), F32),
        pltpu.VMEM((GROUPS, OWN_COLS, OWN_ROWS), F32),
        pltpu.VMEM((OWN_COLS, OWN_ROWS), BF16),
        pltpu.VMEM((SHARDS, OWN_COLS, OWN_ROWS), BF16),
        pltpu.SemaphoreType.DMA((2, CHUNKS)),
        pltpu.SemaphoreType.DMA((2, CHUNKS)),
        pltpu.SemaphoreType.DMA((2,)),
        pltpu.SemaphoreType.DMA((2, GROUPS)),
        pltpu.SemaphoreType.DMA((2,)),
    ]
    return pl.pallas_call(
        kernel,
        out_shape=(
            jax.ShapeDtypeStruct(activations.shape, BF16),
            jax.ShapeDtypeStruct((OWN_ROWS, WIDTH), F32),
        ),
        in_specs=[smem, smem, vmem, vmem, vmem, vmem],
        out_specs=(vmem, vmem),
        scratch_shapes=scratch,
        compiler_params=pltpu.CompilerParams(
            collective_id=0, has_side_effects=True, vmem_limit_bytes=60 << 20
        ),
    )(counts, offsets, activations, out_grad, embedding, layout)


def solution(mesh):
    placed = (
        P("group", "shard", None, None),
        P("group", None, "shard", None),
        P(),
        P("group", None),
        P("group", None),
        P("group", None),
    )
    return jax.shard_map(
        body,
        mesh=mesh,
        in_specs=placed,
        out_specs=(P("group", "shard", None, None), P("group", None)),
        check_vma=False,
    )
```

```python
import functools

import jax
import jax.numpy as jnp
from jax import lax
from jax.experimental import pallas as pl
from jax.experimental.pallas import tpu as pltpu
from jax.sharding import PartitionSpec as P

MESH = pl.DeviceIdType.MESH
SHARDS = 64
GROUPS = 4
HALF = 64
LANES = 128
PAIRS = 8
SLOTS = 256
PATCHES = 128
TEMPLATES = 512
WIDTH = 1024
CHIPS = SHARDS // 2
STAGES = 2
OWN_COLS = WIDTH // SHARDS // STAGES
OWN_ROWS = TEMPLATES // GROUPS
SCALE = 0.0625
BLOCK_SHIFT = 5
SESSIONS = 8
F32 = jnp.float32
BF16 = jnp.bfloat16


def mm(a, b):
    return lax.dot_general(a, b, (((1,), (0,)), ((), ())), preferred_element_type=F32)


def mm_nt(a, b):
    return lax.dot_general(a, b, (((1,), (1,)), ((), ())), preferred_element_type=F32)


def head_masks(values):
    lane = lax.broadcasted_iota(jnp.int32, values.shape, 1)
    zero = jnp.zeros_like(values)
    return jnp.where(lane < HALF, values, zero), jnp.where(lane < HALF, zero, values)


def column_softmax(scores):
    top = jnp.max(scores, axis=0, keepdims=True)
    exponent = jnp.exp(scores - top)
    total = jnp.sum(exponent, axis=0, keepdims=True)
    return (exponent * (1.0 / total)).astype(BF16)


def turned_grad_scores(weights_t, grad_weights_t):
    wide = weights_t.astype(F32)
    row_delta = jnp.sum(wide * grad_weights_t, axis=0, keepdims=True)
    return (wide * (grad_weights_t - row_delta)).astype(BF16)


def spatial_pair(values, bias):
    scaled = values * jnp.asarray(SCALE, BF16)
    values_t = jnp.transpose(values)
    weights, parts = [], []
    for head, masked in enumerate(head_masks(values)):
        scores_t = mm_nt(scaled, masked) + bias
        weights_t = column_softmax(scores_t)
        weights.append(weights_t)
        parts.append(mm(values_t[head * HALF : (head + 1) * HALF], weights_t))
    attended = jnp.transpose(jnp.concatenate(parts, axis=0))
    return values.astype(F32) + attended, weights


def temporal_pair(values, cotangent):
    scaled = values * jnp.asarray(SCALE, BF16)
    scaled_t = jnp.transpose(scaled)
    stacked = jnp.concatenate(head_masks(values), axis=0)
    stacked_grad = jnp.concatenate(head_masks(cotangent), axis=0)
    scores_t = mm_nt(scaled, stacked)
    weights_t = column_softmax(scores_t)
    grad_weights_t = mm_nt(values, stacked_grad)
    grad_scores_t = turned_grad_scores(weights_t, grad_weights_t)
    stacked_scaled = stacked * jnp.asarray(SCALE, BF16)
    direct = mm(grad_scores_t, stacked_scaled) + mm(weights_t, stacked_grad)
    turned = mm(scaled_t, grad_scores_t)
    row = lax.broadcasted_iota(jnp.int32, (LANES, LANES), 0)
    turned = jnp.where(row < HALF, turned[:, :LANES], turned[:, LANES:])
    return cotangent.astype(F32) + direct + jnp.transpose(turned)


def spatial_back_pair(values, weights, cotangent):
    scaled = values * jnp.asarray(SCALE, BF16)
    scaled_t = jnp.transpose(scaled)
    total = cotangent.astype(F32)
    parts = []
    pieces = zip(weights, head_masks(scaled), head_masks(cotangent))
    for head, (weights_t, scaled_head, grad_head) in enumerate(pieces):
        grad_weights_t = mm_nt(values, grad_head)
        grad_scores_t = turned_grad_scores(weights_t, grad_weights_t)
        total = total + (mm(grad_scores_t, scaled_head) + mm(weights_t, grad_head))
        parts.append(mm(scaled_t[head * HALF : (head + 1) * HALF], grad_scores_t))
    return total + jnp.transpose(jnp.concatenate(parts, axis=0))


def weave(first, second, roll):
    columns = first.shape[1]
    first = first.reshape(SLOTS // 8, 8, columns)
    second = second.reshape(SLOTS // 8, 8, columns)
    low = lax.broadcasted_iota(jnp.int32, first.shape, 1) < 4
    even = jnp.where(low, first, roll(second, 4, 1))
    odd = jnp.where(low, roll(first, 4, 1), second)
    return jnp.stack([even, odd], axis=1).reshape(SHARDS, 8, columns)


def unweave(blocks, roll):
    columns = blocks.shape[2]
    blocks = blocks.reshape(SLOTS // 8, 2, 8, columns)
    even, odd = blocks[:, 0], blocks[:, 1]
    low = lax.broadcasted_iota(jnp.int32, even.shape, 1) < 4
    first = jnp.where(low, even, roll(odd, 4, 1))
    second = jnp.where(low, roll(even, 4, 1), odd)
    return first.reshape(SLOTS, columns), second.reshape(SLOTS, columns)


def session_bias(counts, offsets):
    def place(slot):
        block = lax.shift_right_logical(slot, BLOCK_SHIFT)
        start = jnp.zeros_like(slot)
        count = jnp.zeros_like(slot)
        for j in range(SESSIONS):
            reached = block >= offsets[0, j]
            start = jnp.where(reached, offsets[0, j], start)
            count = jnp.where(reached, counts[0, j], count)
        return start, count

    keys = lax.broadcasted_iota(jnp.int32, (SLOTS, LANES), 0)
    key_start, key_count = place(keys)
    live = keys - (1 << BLOCK_SHIFT) * key_start < key_count
    key_start = jnp.where(live, key_start, -1)
    halves = []
    for half in range(SLOTS // LANES):
        queries = lax.broadcasted_iota(jnp.int32, (SLOTS, LANES), 1) + half * LANES
        query_start, _ = place(queries)
        halves.append(jnp.where(query_start == key_start, 0.0, -1e30))
    return jnp.concatenate(halves, axis=1)


def kernel(
    counts,
    offsets,
    act_hbm,
    out_grad_hbm,
    table_hbm,
    layout,
    input_grad,
    table_grad,
    act,
    out_grad,
    table,
    embedded,
    saved,
    bias,
    chosen,
    rows_in,
    rows_grad,
    rows_out,
    send_mix,
    recv_mix,
    send_back,
    recv_back,
    partial,
    recv_pair,
    summed,
    recv_sum,
    send_group,
    recv_group,
    send_part,
    recv_part,
    load_sems,
    mix_sems,
    back_sems,
    pair_sems,
    sum_sems,
    group_sems,
    part_sems,
):
    me = lax.axis_index("shard")
    group = lax.axis_index("group")
    chip = me // 2
    core = lax.rem(me, 2)
    partner = me + 1 - 2 * core

    loads = [
        pltpu.make_async_copy(act_hbm, act, load_sems.at[0]),
        pltpu.make_async_copy(table_hbm, table, load_sems.at[1]),
        pltpu.make_async_copy(out_grad_hbm, out_grad, load_sems.at[2]),
    ]
    for load in loads:
        load.start()

    barrier = pltpu.get_barrier_semaphore()

    @pl.loop(1, SHARDS)
    def _(step):
        peer = lax.rem(me + step, SHARDS)
        pl.semaphore_signal(barrier, inc=1, device_id=(group, peer), device_id_type=MESH)

    for step in range(1, GROUPS):
        other = lax.rem(group + step, GROUPS)
        pl.semaphore_signal(barrier, inc=1, device_id=(other, me), device_id_type=MESH)

    bias[...] = session_bias(counts, offsets)
    template = lax.broadcasted_iota(jnp.int32, (TEMPLATES, SLOTS), 0)
    hit = jnp.where(template == layout[...], 1.0, 0.0)
    chosen[...] = jnp.transpose(hit).astype(BF16)

    def remote(source, target, sems, at, peer):
        return pltpu.make_async_remote_copy(
            src_ref=source,
            dst_ref=target,
            send_sem=sems.at[(0, *at)],
            recv_sem=sems.at[(1, *at)],
            device_id=peer,
            device_id_type=MESH,
        )

    def spread(source, target, sems, pair):
        @pl.loop(1, SHARDS)
        def _(step):
            peer = lax.rem(me + step, SHARDS)
            remote(
                source.at[pair, peer], target.at[pair, me], sems, (pair,), (group, peer)
            ).start()

        target[pair, me] = source[pair, me]

    def several(buffer, count, sems, at):
        whole = buffer.at[pl.ds(0, count)]
        return remote(whole, whole, sems, at, (group, partner))

    def spatial_step(pair):
        lanes = pl.ds(pl.multiple_of(pair * LANES, LANES), LANES)
        rows = mm(chosen[...], table[:, lanes])
        mixed = []
        for patch in range(2):
            values = (act[0, patch, :, lanes].astype(F32) + rows).astype(BF16)
            embedded[patch, pair] = values
            out, weights = spatial_pair(values, bias[...])
            for head in range(2):
                saved[patch, pair, head] = weights[head]
            mixed.append(out)
        send_mix[pair] = weave(mixed[0], mixed[1], pltpu.roll).astype(BF16)

    def temporal_step(pair):
        lanes = pl.ds(pl.multiple_of(pair * LANES, LANES), LANES)
        rows_in[...] = recv_mix[pair].astype(F32).reshape(PATCHES * 4, LANES)
        rows_grad[:, 0:4, :] = out_grad[0, :, :, lanes].astype(F32)
        flat_grad = rows_grad.reshape(PATCHES * 8, LANES)
        for slot in range(4):
            values = rows_in[pl.ds(slot, PATCHES, stride=4), :].astype(BF16)
            cotangent = flat_grad[pl.ds(slot, PATCHES, stride=8), :].astype(BF16)
            rows_out[pl.ds(slot, PATCHES, stride=4), :] = temporal_pair(values, cotangent)
        send_back[pair] = rows_out[...].reshape(SHARDS, 8, LANES).astype(BF16)

    def back_step(pair):
        lanes = pl.ds(pl.multiple_of(pair * LANES, LANES), LANES)
        grads = unweave(recv_back[pair].astype(F32), pltpu.roll)
        electrode = None
        for patch in range(2):
            full = spatial_back_pair(
                embedded[patch, pair],
                [saved[patch, pair, head] for head in range(2)],
                grads[patch].astype(BF16),
            )
            input_grad[0, patch, :, lanes] = full.astype(BF16)
            electrode = full if electrode is None else electrode + full
        blocks = jnp.transpose(electrode).reshape(LANES // OWN_COLS, OWN_COLS, SLOTS)
        partial[pair] = blocks.astype(BF16)

    half = LANES // OWN_COLS

    def exchange_cores(duo):
        return remote(
            partial.at[2 * duo + 1 - core],
            recv_pair.at[duo],
            pair_sems,
            (duo,),
            (group, partner),
        )

    def sum_cores(stage):
        for part in range(2):
            duo = 2 * stage + part
            exchange_cores(duo).wait_recv()
            own = partial[2 * duo + core].astype(F32)
            both = own + recv_pair[duo].astype(F32)
            summed[stage, part * half : (part + 1) * half] = both.astype(BF16)

        @pl.loop(1, CHIPS)
        def _(step):
            peer = lax.rem(chip + step, CHIPS)
            remote(
                summed.at[stage, peer],
                recv_sum.at[stage, chip],
                sum_sems,
                (stage,),
                (group, 2 * peer + core),
            ).start()

        recv_sum[stage, chip] = summed[stage, chip]

    def group_copies(stage):
        copies = []
        for step in range(1, GROUPS):
            other = lax.rem(group + step, GROUPS)
            copies.append(
                remote(
                    send_group.at[stage, other],
                    recv_group.at[stage, step],
                    group_sems,
                    (stage, step),
                    (other, me),
                )
            )
        return copies

    def sum_chips(stage):
        several(recv_sum.at[stage], CHIPS - 1, sum_sems, (stage,)).wait_recv()
        columns = jnp.sum(recv_sum[stage].astype(F32), axis=0)
        high = columns.astype(BF16)
        low = (columns - high.astype(F32)).astype(BF16)
        both = mm(jnp.concatenate([high, low], axis=0), chosen[...])
        own = both[:OWN_COLS] + both[OWN_COLS:]
        for other in range(GROUPS):
            rows = own[:, other * OWN_ROWS : (other + 1) * OWN_ROWS]
            send_group[stage, other] = rows
        for copy in group_copies(stage):
            copy.start()

    def sum_groups(stage):
        part = send_group[stage, group]
        for step, copy in enumerate(group_copies(stage)):
            copy.wait_recv()
            part = part + recv_group[stage, step + 1]
        part = part.astype(BF16)
        send_part[stage] = part
        slot = (2 * (chip // half) + core) * half + lax.rem(chip, half)

        @pl.loop(1, SHARDS)
        def _(step):
            peer = lax.rem(me + step, SHARDS)
            remote(
                send_part.at[stage],
                recv_part.at[stage, slot],
                part_sems,
                (stage,),
                (group, peer),
            ).start()

        recv_part[stage, slot] = part

    def write_table(stage):
        several(recv_part.at[stage], SHARDS - 1, part_sems, (stage,)).wait_recv()
        columns = WIDTH // STAGES
        turned = recv_part[stage].astype(F32).reshape(columns, OWN_ROWS)
        table_grad[:, stage * columns : (stage + 1) * columns] = jnp.transpose(turned)

    loads[0].wait()
    loads[1].wait()
    spatial_step(0)
    pl.semaphore_wait(barrier, SHARDS - 1 + GROUPS - 1)
    spread(send_mix, recv_mix, mix_sems, 0)

    @pl.loop(1, PAIRS)
    def _(pair):
        spatial_step(pair)
        spread(send_mix, recv_mix, mix_sems, pair)

    loads[2].wait()

    @pl.loop(0, PAIRS)
    def _(pair):
        several(recv_mix.at[pair], SHARDS - 1, mix_sems, (pair,)).wait_recv()
        temporal_step(pair)
        spread(send_back, recv_back, back_sems, pair)

    @pl.loop(0, PAIRS)
    def _(pair):
        several(recv_back.at[pair], SHARDS - 1, back_sems, (pair,)).wait_recv()
        back_step(pair)

        @pl.when(lax.rem(pair, 2) == 1)
        def _():
            exchange_cores(pair // 2).start()

        @pl.when(pair == 4)
        def _():
            sum_cores(0)

        @pl.when(pair == 6)
        def _():
            sum_chips(0)

    sum_groups(0)
    sum_cores(1)
    write_table(0)
    sum_chips(1)
    sum_groups(1)
    write_table(1)

    @pl.loop(0, PAIRS)
    def _(pair):
        several(send_mix.at[pair], SHARDS - 1, mix_sems, (pair,)).wait_send()
        several(send_back.at[pair], SHARDS - 1, back_sems, (pair,)).wait_send()

    for duo in range(PAIRS // 2):
        exchange_cores(duo).wait_send()
    for stage in range(STAGES):
        several(summed.at[stage], CHIPS - 1, sum_sems, (stage,)).wait_send()
        several(recv_part.at[stage], SHARDS - 1, part_sems, (stage,)).wait_send()
        for copy in group_copies(stage):
            copy.wait_send()


def body(activations, out_grad, embedding, counts, offsets, layout):
    vmem = pl.BlockSpec(memory_space=pltpu.VMEM)
    smem = pl.BlockSpec(memory_space=pltpu.SMEM)
    hbm = pl.BlockSpec(memory_space=pltpu.HBM)
    blocks = pltpu.VMEM((PAIRS, SHARDS, 8, LANES), BF16)
    halves = LANES // OWN_COLS
    scratch = [
        pltpu.VMEM(activations.shape, BF16),
        pltpu.VMEM(out_grad.shape, BF16),
        pltpu.VMEM(embedding.shape, BF16),
        pltpu.VMEM((2, PAIRS, SLOTS, LANES), BF16),
        pltpu.VMEM((2, PAIRS, 2, SLOTS, SLOTS), BF16),
        pltpu.VMEM((SLOTS, SLOTS), F32),
        pltpu.VMEM((SLOTS, TEMPLATES), BF16),
        pltpu.VMEM((PATCHES * 4, LANES), F32),
        pltpu.VMEM((PATCHES, 8, LANES), F32),
        pltpu.VMEM((PATCHES * 4, LANES), F32),
        blocks,
        blocks,
        blocks,
        blocks,
        pltpu.VMEM((PAIRS, halves, OWN_COLS, SLOTS), BF16),
        pltpu.VMEM((PAIRS // 2, halves, OWN_COLS, SLOTS), BF16),
        pltpu.VMEM((STAGES, CHIPS, OWN_COLS, SLOTS), BF16),
        pltpu.VMEM((STAGES, CHIPS, OWN_COLS, SLOTS), BF16),
        pltpu.VMEM((STAGES, GROUPS, OWN_COLS, OWN_ROWS), F32),
        pltpu.VMEM((STAGES, GROUPS, OWN_COLS, OWN_ROWS), F32),
        pltpu.VMEM((STAGES, OWN_COLS, OWN_ROWS), BF16),
        pltpu.VMEM((STAGES, SHARDS, OWN_COLS, OWN_ROWS), BF16),
        pltpu.SemaphoreType.DMA((3,)),
        pltpu.SemaphoreType.DMA((2, PAIRS)),
        pltpu.SemaphoreType.DMA((2, PAIRS)),
        pltpu.SemaphoreType.DMA((2, PAIRS // 2)),
        pltpu.SemaphoreType.DMA((2, STAGES)),
        pltpu.SemaphoreType.DMA((2, STAGES, GROUPS)),
        pltpu.SemaphoreType.DMA((2, STAGES)),
    ]
    return pl.pallas_call(
        kernel,
        out_shape=(
            pltpu.VMEM(activations.shape, BF16),
            pltpu.VMEM((OWN_ROWS, WIDTH), F32),
        ),
        in_specs=[smem, smem, hbm, hbm, hbm, vmem],
        out_specs=(vmem, vmem),
        scratch_shapes=scratch,
        compiler_params=pltpu.CompilerParams(
            collective_id=0, has_side_effects=True, vmem_limit_bytes=56 << 20
        ),
    )(counts, offsets, activations, out_grad, embedding, layout)


def solution(mesh):
    placed = (
        P("group", "shard", None, None),
        P("group", None, "shard", None),
        P(),
        P("group", None),
        P("group", None),
        P("group", None),
    )
    return jax.shard_map(
        body,
        mesh=mesh,
        in_specs=placed,
        out_specs=(P("group", "shard", None, None), P("group", None)),
        check_vma=False,
    )
```

```python
import functools

import jax
import jax.numpy as jnp
from jax import lax
from jax.experimental import pallas as pl
from jax.experimental.pallas import tpu as pltpu
from jax.sharding import PartitionSpec as P

MESH = pl.DeviceIdType.MESH
SHARDS = 64
GROUPS = 4
HALF = 64
LANES = 128
PAIRS = 8
SLOTS = 256
PATCHES = 128
TEMPLATES = 512
WIDTH = 1024
LINE = 8
DEPTH = 8
DUOS = PAIRS // 2
SLICE = 32
STAGES = ((0, 3), (3, 1))
OWN_ROWS = TEMPLATES // GROUPS
SCALE = 0.0625
BLOCK_SHIFT = 5
SESSIONS = 8
F32 = jnp.float32
BF16 = jnp.bfloat16


def mm(a, b):
    return lax.dot_general(a, b, (((1,), (0,)), ((), ())), preferred_element_type=F32)


def mm_nt(a, b):
    return lax.dot_general(a, b, (((1,), (1,)), ((), ())), preferred_element_type=F32)


def head_masks(values):
    lane = lax.broadcasted_iota(jnp.int32, values.shape, 1)
    zero = jnp.zeros_like(values)
    return jnp.where(lane < HALF, values, zero), jnp.where(lane < HALF, zero, values)


def column_softmax(scores):
    top = jnp.max(scores, axis=0, keepdims=True)
    exponent = jnp.exp(scores - top)
    total = jnp.sum(exponent, axis=0, keepdims=True)
    return (exponent * (1.0 / total)).astype(BF16)


def turned_grad_scores(weights_t, grad_weights_t):
    wide = weights_t.astype(F32)
    row_delta = jnp.sum(wide * grad_weights_t, axis=0, keepdims=True)
    return (wide * (grad_weights_t - row_delta)).astype(BF16)


def spatial_pair(values, bias):
    scaled = values * jnp.asarray(SCALE, BF16)
    values_t = jnp.transpose(values)
    weights, parts = [], []
    for head, masked in enumerate(head_masks(values)):
        scores_t = mm_nt(scaled, masked) + bias
        weights_t = column_softmax(scores_t)
        weights.append(weights_t)
        parts.append(mm(values_t[head * HALF : (head + 1) * HALF], weights_t))
    attended = jnp.transpose(jnp.concatenate(parts, axis=0))
    return values.astype(F32) + attended, weights


def temporal_pair(values, cotangent):
    scaled = values * jnp.asarray(SCALE, BF16)
    scaled_t = jnp.transpose(scaled)
    stacked = jnp.concatenate(head_masks(values), axis=0)
    stacked_grad = jnp.concatenate(head_masks(cotangent), axis=0)
    scores_t = mm_nt(scaled, stacked)
    weights_t = column_softmax(scores_t)
    grad_weights_t = mm_nt(values, stacked_grad)
    grad_scores_t = turned_grad_scores(weights_t, grad_weights_t)
    stacked_scaled = stacked * jnp.asarray(SCALE, BF16)
    direct = mm(grad_scores_t, stacked_scaled) + mm(weights_t, stacked_grad)
    turned = mm(scaled_t, grad_scores_t)
    row = lax.broadcasted_iota(jnp.int32, (LANES, LANES), 0)
    turned = jnp.where(row < HALF, turned[:, :LANES], turned[:, LANES:])
    return cotangent.astype(F32) + direct + jnp.transpose(turned)


def spatial_back_pair(values, weights, cotangent):
    scaled = values * jnp.asarray(SCALE, BF16)
    scaled_t = jnp.transpose(scaled)
    total = cotangent.astype(F32)
    parts = []
    pieces = zip(weights, head_masks(scaled), head_masks(cotangent))
    for head, (weights_t, scaled_head, grad_head) in enumerate(pieces):
        grad_weights_t = mm_nt(values, grad_head)
        grad_scores_t = turned_grad_scores(weights_t, grad_weights_t)
        total = total + (mm(grad_scores_t, scaled_head) + mm(weights_t, grad_head))
        parts.append(mm(scaled_t[head * HALF : (head + 1) * HALF], grad_scores_t))
    return total + jnp.transpose(jnp.concatenate(parts, axis=0))


def weave(first, second, roll):
    columns = first.shape[1]
    first = first.reshape(SLOTS // 8, 8, columns)
    second = second.reshape(SLOTS // 8, 8, columns)
    low = lax.broadcasted_iota(jnp.int32, first.shape, 1) < 4
    even = jnp.where(low, first, roll(second, 4, 1))
    odd = jnp.where(low, roll(first, 4, 1), second)
    return jnp.stack([even, odd], axis=1).reshape(SHARDS, 8, columns)


def unweave(blocks, roll):
    columns = blocks.shape[2]
    blocks = blocks.reshape(SLOTS // 8, 2, 8, columns)
    even, odd = blocks[:, 0], blocks[:, 1]
    low = lax.broadcasted_iota(jnp.int32, even.shape, 1) < 4
    first = jnp.where(low, even, roll(odd, 4, 1))
    second = jnp.where(low, roll(even, 4, 1), odd)
    return first.reshape(SLOTS, columns), second.reshape(SLOTS, columns)


def session_bias(counts, offsets):
    def place(slot):
        block = lax.shift_right_logical(slot, BLOCK_SHIFT)
        start = jnp.zeros_like(slot)
        count = jnp.zeros_like(slot)
        for j in range(SESSIONS):
            reached = block >= offsets[0, j]
            start = jnp.where(reached, offsets[0, j], start)
            count = jnp.where(reached, counts[0, j], count)
        return start, count

    keys = lax.broadcasted_iota(jnp.int32, (SLOTS, LANES), 0)
    key_start, key_count = place(keys)
    live = keys - (1 << BLOCK_SHIFT) * key_start < key_count
    key_start = jnp.where(live, key_start, -1)
    halves = []
    for half in range(SLOTS // LANES):
        queries = lax.broadcasted_iota(jnp.int32, (SLOTS, LANES), 1) + half * LANES
        query_start, _ = place(queries)
        halves.append(jnp.where(query_start == key_start, 0.0, -1e30))
    return jnp.concatenate(halves, axis=1)


def kernel(
    counts,
    offsets,
    act_hbm,
    out_grad_hbm,
    table_hbm,
    layout,
    input_grad,
    table_grad,
    act,
    out_grad,
    table,
    embedded,
    saved,
    bias,
    chosen,
    rows_in,
    rows_grad,
    rows_out,
    send_mix,
    recv_mix,
    send_back,
    recv_back,
    partial,
    recv_line,
    send_group,
    recv_group,
    send_depth,
    recv_depth,
    send_last,
    recv_last,
    load_sems,
    mix_sems,
    back_sems,
    line_sems,
    group_sems,
    depth_sems,
    last_sems,
):
    me = lax.axis_index("shard")
    group = lax.axis_index("group")
    core = lax.rem(me, 2)
    across = me // 16
    deep = lax.rem(me // 2, DEPTH)
    line = across * 2 + core

    loads = [
        pltpu.make_async_copy(act_hbm, act, load_sems.at[0]),
        pltpu.make_async_copy(table_hbm, table, load_sems.at[1]),
        pltpu.make_async_copy(out_grad_hbm, out_grad, load_sems.at[2]),
    ]
    for load in loads:
        load.start()

    barrier = pltpu.get_barrier_semaphore()

    def beside(step):
        return lax.rem(me + 16 * step, SHARDS)

    @pl.loop(1, SHARDS)
    def _(step):
        peer = lax.rem(me + step, SHARDS)
        pl.semaphore_signal(barrier, inc=1, device_id=(group, peer), device_id_type=MESH)

    for step in range(1, GROUPS):
        other = lax.rem(group + step, GROUPS)
        pl.semaphore_signal(barrier, inc=1, device_id=(other, me), device_id_type=MESH)

    bias[...] = session_bias(counts, offsets)
    template = lax.broadcasted_iota(jnp.int32, (TEMPLATES, SLOTS), 0)
    hit = jnp.where(template == layout[...], 1.0, 0.0)
    chosen[...] = jnp.transpose(hit).astype(BF16)

    def remote(source, target, sems, at, peer):
        return pltpu.make_async_remote_copy(
            src_ref=source,
            dst_ref=target,
            send_sem=sems.at[(0, *at)],
            recv_sem=sems.at[(1, *at)],
            device_id=peer,
            device_id_type=MESH,
        )

    def spread(source, target, sems, pair):
        @pl.loop(1, SHARDS)
        def _(step):
            peer = lax.rem(me + SHARDS - step, SHARDS)
            remote(
                source.at[pair, peer], target.at[pair, me], sems, (pair,), (group, peer)
            ).start()

        target[pair, me] = source[pair, me]

    def several(buffer, count, sems, at):
        whole = buffer.at[pl.ds(0, count)]
        return remote(whole, whole, sems, at, (group, beside(1)))

    def spatial_step(pair):
        lanes = pl.ds(pl.multiple_of(pair * LANES, LANES), LANES)
        rows = mm(chosen[...], table[:, lanes])
        mixed = []
        for patch in range(2):
            values = (act[0, patch, :, lanes].astype(F32) + rows).astype(BF16)
            embedded[patch, pair] = values
            out, weights = spatial_pair(values, bias[...])
            for head in range(2):
                saved[patch, pair, head] = weights[head]
            mixed.append(out)
        send_mix[pair] = weave(mixed[0], mixed[1], pltpu.roll).astype(BF16)

    def temporal_step(pair):
        lanes = pl.ds(pl.multiple_of(pair * LANES, LANES), LANES)
        rows_in[...] = recv_mix[pair].astype(F32).reshape(PATCHES * 4, LANES)
        rows_grad[:, 0:4, :] = out_grad[0, :, :, lanes].astype(F32)
        flat_grad = rows_grad.reshape(PATCHES * 8, LANES)
        for slot in range(4):
            values = rows_in[pl.ds(slot, PATCHES, stride=4), :].astype(BF16)
            cotangent = flat_grad[pl.ds(slot, PATCHES, stride=8), :].astype(BF16)
            rows_out[pl.ds(slot, PATCHES, stride=4), :] = temporal_pair(values, cotangent)
        send_back[pair] = rows_out[...].reshape(SHARDS, 8, LANES).astype(BF16)

    def back_step(pair):
        lanes = pl.ds(pl.multiple_of(pair * LANES, LANES), LANES)
        grads = unweave(recv_back[pair].astype(F32), pltpu.roll)
        electrode = None
        for patch in range(2):
            full = spatial_back_pair(
                embedded[patch, pair],
                [saved[patch, pair, head] for head in range(2)],
                grads[patch].astype(BF16),
            )
            input_grad[0, patch, :, lanes] = full.astype(BF16)
            electrode = full if electrode is None else electrode + full
        turned = jnp.transpose(electrode).astype(BF16)
        partial[pair] = turned.reshape(LANES // SLICE, SLICE, SLOTS)

    def on_line(step):
        other = lax.rem(line + step, LINE)
        return other, (group, (other // 2) * 16 + deep * 2 + lax.rem(other, 2))

    def send_line(duo):
        for step in range(1, LINE):
            other, peer = on_line(step)
            block = partial.at[2 * duo + lax.rem(other, 2), other // 2]
            remote(block, recv_line.at[duo, line], line_sems, (duo,), peer).start()
        recv_line[duo, line] = partial[2 * duo + core, across]

    def group_copies(stage):
        first, count = STAGES[stage]
        span = pl.ds(first, count)
        copies = []
        for step in range(1, GROUPS):
            other = lax.rem(group + step, GROUPS)
            source, target = send_group.at[other, span], recv_group.at[step, span]
            copies.append(remote(source, target, group_sems, (stage, step), (other, me)))
        return copies

    def sum_line(stage):
        first, count = STAGES[stage]
        highs, lows = [], []
        for duo in range(first, first + count):
            several(recv_line.at[duo], LINE - 1, line_sems, (duo,)).wait_recv()
            columns = jnp.sum(recv_line[duo].astype(F32), axis=0)
            high = columns.astype(BF16)
            highs.append(high)
            lows.append((columns - high.astype(F32)).astype(BF16))
        both = mm(jnp.concatenate(highs + lows, axis=0), chosen[...])
        own = (both[: count * SLICE] + both[count * SLICE :]).astype(BF16)
        for other in range(GROUPS):
            rows = own[:, other * OWN_ROWS : (other + 1) * OWN_ROWS]
            send_group[other, first : first + count] = rows.reshape(count, SLICE, OWN_ROWS)
        for copy in group_copies(stage):
            copy.start()

    def sum_groups(stage):
        first, count = STAGES[stage]
        span = pl.ds(first, count)
        part = send_group[group, span].astype(F32)
        for step, copy in enumerate(group_copies(stage)):
            copy.wait_recv()
            part = part + recv_group[step + 1, span].astype(F32)
        send_depth[span] = part.astype(BF16)
        for step in range(1, DEPTH):
            peer = (group, across * 16 + lax.rem(deep + step, DEPTH) * 2 + core)
            target = recv_depth.at[deep, span]
            remote(send_depth.at[span], target, depth_sems, (stage,), peer).start()
        recv_depth[deep, span] = part.astype(BF16)

    def wide(buffer, stage):
        first, count = STAGES[stage]
        return buffer.at[:, pl.ds(first, count)]

    def sum_depth(stage):
        first, count = STAGES[stage]
        span = pl.ds(first, count)
        several(wide(recv_depth, stage), DEPTH - 1, depth_sems, (stage,)).wait_recv()
        total = recv_depth[0, span].astype(F32)
        for other in range(1, DEPTH):
            total = total + recv_depth[other, span].astype(F32)
        send_last[span] = total.astype(BF16)
        for step in range(1, LINE):
            _, peer = on_line(step)
            target = recv_last.at[line, span]
            remote(send_last.at[span], target, last_sems, (stage,), peer).start()
        recv_last[line, span] = total.astype(BF16)

    def write_table(stage):
        first, count = STAGES[stage]
        several(wide(recv_last, stage), LINE - 1, last_sems, (stage,)).wait_recv()
        for duo in range(first, first + count):
            for side in range(2):
                parts = [recv_last[2 * k + side, duo] for k in range(LANES // SLICE)]
                turned = jnp.transpose(jnp.concatenate(parts, axis=0).astype(F32))
                start = (2 * duo + side) * LANES
                table_grad[:, start : start + LANES] = turned

    loads[0].wait()
    loads[1].wait()

    spatial_step(0)
    pl.semaphore_wait(barrier, SHARDS - 1 + GROUPS - 1)
    spread(send_mix, recv_mix, mix_sems, 0)

    @pl.loop(1, PAIRS)
    def _(pair):
        spatial_step(pair)
        spread(send_mix, recv_mix, mix_sems, pair)

    loads[2].wait()

    @pl.loop(0, PAIRS)
    def _(pair):
        several(recv_mix.at[pair], SHARDS - 1, mix_sems, (pair,)).wait_recv()
        temporal_step(pair)
        spread(send_back, recv_back, back_sems, pair)

    @pl.loop(0, PAIRS)
    def _(pair):
        several(recv_back.at[pair], SHARDS - 1, back_sems, (pair,)).wait_recv()
        back_step(pair)

        @pl.when(lax.rem(pair, 2) == 1)
        def _():
            send_line(pair // 2)

        @pl.when(pair == 6)
        def _():
            sum_line(0)

    sum_groups(0)
    sum_line(1)
    sum_groups(1)
    sum_depth(0)
    sum_depth(1)
    write_table(0)
    write_table(1)

    @pl.loop(0, PAIRS)
    def _(pair):
        several(send_mix.at[pair], SHARDS - 1, mix_sems, (pair,)).wait_send()
        several(send_back.at[pair], SHARDS - 1, back_sems, (pair,)).wait_send()

    for duo in range(DUOS):
        several(recv_line.at[duo], LINE - 1, line_sems, (duo,)).wait_send()
    for stage in range(len(STAGES)):
        several(wide(recv_depth, stage), DEPTH - 1, depth_sems, (stage,)).wait_send()
        several(wide(recv_last, stage), LINE - 1, last_sems, (stage,)).wait_send()
        for copy in group_copies(stage):
            copy.wait_send()


def body(activations, out_grad, embedding, counts, offsets, layout):
    vmem = pl.BlockSpec(memory_space=pltpu.VMEM)
    smem = pl.BlockSpec(memory_space=pltpu.SMEM)
    hbm = pl.BlockSpec(memory_space=pltpu.HBM)
    blocks = pltpu.VMEM((PAIRS, SHARDS, 8, LANES), BF16)
    slices = LANES // SLICE
    rows = (DUOS, SLICE, OWN_ROWS)
    scratch = [
        pltpu.VMEM(activations.shape, BF16),
        pltpu.VMEM(out_grad.shape, BF16),
        pltpu.VMEM(embedding.shape, BF16),
        pltpu.VMEM((2, PAIRS, SLOTS, LANES), BF16),
        pltpu.VMEM((2, PAIRS, 2, SLOTS, SLOTS), BF16),
        pltpu.VMEM((SLOTS, SLOTS), F32),
        pltpu.VMEM((SLOTS, TEMPLATES), BF16),
        pltpu.VMEM((PATCHES * 4, LANES), F32),
        pltpu.VMEM((PATCHES, 8, LANES), F32),
        pltpu.VMEM((PATCHES * 4, LANES), F32),
        blocks,
        blocks,
        blocks,
        blocks,
        pltpu.VMEM((PAIRS, slices, SLICE, SLOTS), BF16),
        pltpu.VMEM((DUOS, LINE, SLICE, SLOTS), BF16),
        pltpu.VMEM((GROUPS, *rows), BF16),
        pltpu.VMEM((GROUPS, *rows), BF16),
        pltpu.VMEM(rows, BF16),
        pltpu.VMEM((DEPTH, *rows), BF16),
        pltpu.VMEM(rows, BF16),
        pltpu.VMEM((LINE, *rows), BF16),
        pltpu.SemaphoreType.DMA((3,)),
        pltpu.SemaphoreType.DMA((2, PAIRS)),
        pltpu.SemaphoreType.DMA((2, PAIRS)),
        pltpu.SemaphoreType.DMA((2, DUOS)),
        pltpu.SemaphoreType.DMA((2, len(STAGES), GROUPS)),
        pltpu.SemaphoreType.DMA((2, len(STAGES))),
        pltpu.SemaphoreType.DMA((2, len(STAGES))),
    ]
    return pl.pallas_call(
        kernel,
        out_shape=(
            pltpu.VMEM(activations.shape, BF16),
            pltpu.VMEM((OWN_ROWS, WIDTH), F32),
        ),
        in_specs=[smem, smem, hbm, hbm, hbm, vmem],
        out_specs=(vmem, vmem),
        scratch_shapes=scratch,
        compiler_params=pltpu.CompilerParams(
            collective_id=0, has_side_effects=True, vmem_limit_bytes=56 << 20
        ),
    )(counts, offsets, activations, out_grad, embedding, layout)


def solution(mesh):
    placed = (
        P("group", "shard", None, None),
        P("group", None, "shard", None),
        P(),
        P("group", None),
        P("group", None),
        P("group", None),
    )
    return jax.shard_map(
        body,
        mesh=mesh,
        in_specs=placed,
        out_specs=(P("group", "shard", None, None), P("group", None)),
        check_vma=False,
    )
```

```python
import functools

import jax
import jax.numpy as jnp
from jax import lax
from jax.experimental import pallas as pl
from jax.experimental.pallas import tpu as pltpu
from jax.sharding import PartitionSpec as P

MESH = pl.DeviceIdType.MESH
SHARDS = 64
GROUPS = 4
HALF = 64
LANES = 128
PAIRS = 8
SLOTS = 256
PATCHES = 128
TEMPLATES = 512
WIDTH = 1024
LINE = 8
DEPTH = 8
DUOS = PAIRS // 2
SLICE = 32
STAGES = ((0, 3), (3, 1))
OWN_ROWS = TEMPLATES // GROUPS
SCALE = 0.0625
BLOCK_SHIFT = 5
SESSIONS = 8
F32 = jnp.float32
BF16 = jnp.bfloat16


def mm(a, b):
    return lax.dot_general(a, b, (((1,), (0,)), ((), ())), preferred_element_type=F32)


def mm_nt(a, b):
    return lax.dot_general(a, b, (((1,), (1,)), ((), ())), preferred_element_type=F32)


def head_masks(values):
    lane = lax.broadcasted_iota(jnp.int32, values.shape, 1)
    zero = jnp.zeros_like(values)
    return jnp.where(lane < HALF, values, zero), jnp.where(lane < HALF, zero, values)


def column_softmax(scores):
    top = jnp.max(scores, axis=0, keepdims=True)
    exponent = jnp.exp(scores - top)
    total = jnp.sum(exponent, axis=0, keepdims=True)
    return (exponent * (1.0 / total)).astype(BF16)


def turned_grad_scores(weights_t, grad_weights_t):
    wide = weights_t.astype(F32)
    row_delta = jnp.sum(wide * grad_weights_t, axis=0, keepdims=True)
    return (wide * (grad_weights_t - row_delta)).astype(BF16)


def spatial_pair(values, bias):
    scaled = values * jnp.asarray(SCALE, BF16)
    values_t = jnp.transpose(values)
    weights, parts = [], []
    for head, masked in enumerate(head_masks(values)):
        scores_t = mm_nt(scaled, masked) + bias
        weights_t = column_softmax(scores_t)
        weights.append(weights_t)
        parts.append(mm(values_t[head * HALF : (head + 1) * HALF], weights_t))
    attended = jnp.transpose(jnp.concatenate(parts, axis=0))
    return values.astype(F32) + attended, weights


def temporal_pair(values, cotangent):
    scaled = values * jnp.asarray(SCALE, BF16)
    scaled_t = jnp.transpose(scaled)
    stacked = jnp.concatenate(head_masks(values), axis=0)
    stacked_grad = jnp.concatenate(head_masks(cotangent), axis=0)
    scores_t = mm_nt(scaled, stacked)
    weights_t = column_softmax(scores_t)
    grad_weights_t = mm_nt(values, stacked_grad)
    grad_scores_t = turned_grad_scores(weights_t, grad_weights_t)
    stacked_scaled = stacked * jnp.asarray(SCALE, BF16)
    direct = mm(grad_scores_t, stacked_scaled) + mm(weights_t, stacked_grad)
    turned = mm(scaled_t, grad_scores_t)
    row = lax.broadcasted_iota(jnp.int32, (LANES, LANES), 0)
    turned = jnp.where(row < HALF, turned[:, :LANES], turned[:, LANES:])
    return cotangent.astype(F32) + direct + jnp.transpose(turned)


def spatial_back_pair(values, weights, cotangent):
    scaled = values * jnp.asarray(SCALE, BF16)
    scaled_t = jnp.transpose(scaled)
    total = cotangent.astype(F32)
    parts = []
    pieces = zip(weights, head_masks(scaled), head_masks(cotangent))
    for head, (weights_t, scaled_head, grad_head) in enumerate(pieces):
        grad_weights_t = mm_nt(values, grad_head)
        grad_scores_t = turned_grad_scores(weights_t, grad_weights_t)
        total = total + (mm(grad_scores_t, scaled_head) + mm(weights_t, grad_head))
        parts.append(mm(scaled_t[head * HALF : (head + 1) * HALF], grad_scores_t))
    return total + jnp.transpose(jnp.concatenate(parts, axis=0))


def weave(first, second, roll):
    columns = first.shape[1]
    first = first.reshape(SLOTS // 8, 8, columns)
    second = second.reshape(SLOTS // 8, 8, columns)
    low = lax.broadcasted_iota(jnp.int32, first.shape, 1) < 4
    even = jnp.where(low, first, roll(second, 4, 1))
    odd = jnp.where(low, roll(first, 4, 1), second)
    return jnp.stack([even, odd], axis=1).reshape(SHARDS, 8, columns)


def unweave(blocks, roll):
    columns = blocks.shape[2]
    blocks = blocks.reshape(SLOTS // 8, 2, 8, columns)
    even, odd = blocks[:, 0], blocks[:, 1]
    low = lax.broadcasted_iota(jnp.int32, even.shape, 1) < 4
    first = jnp.where(low, even, roll(odd, 4, 1))
    second = jnp.where(low, roll(even, 4, 1), odd)
    return first.reshape(SLOTS, columns), second.reshape(SLOTS, columns)


def session_bias(counts, offsets):
    def place(slot):
        block = lax.shift_right_logical(slot, BLOCK_SHIFT)
        start = jnp.zeros_like(slot)
        count = jnp.zeros_like(slot)
        for j in range(SESSIONS):
            reached = block >= offsets[0, j]
            start = jnp.where(reached, offsets[0, j], start)
            count = jnp.where(reached, counts[0, j], count)
        return start, count

    keys = lax.broadcasted_iota(jnp.int32, (SLOTS, LANES), 0)
    key_start, key_count = place(keys)
    live = keys - (1 << BLOCK_SHIFT) * key_start < key_count
    key_start = jnp.where(live, key_start, -1)
    halves = []
    for half in range(SLOTS // LANES):
        queries = lax.broadcasted_iota(jnp.int32, (SLOTS, LANES), 1) + half * LANES
        query_start, _ = place(queries)
        halves.append(jnp.where(query_start == key_start, 0.0, -1e30))
    return jnp.concatenate(halves, axis=1)


def kernel(
    counts,
    offsets,
    act_hbm,
    out_grad_hbm,
    table_hbm,
    layout,
    input_grad,
    table_grad,
    act,
    out_grad,
    table,
    embedded,
    saved,
    bias,
    chosen,
    rows_in,
    rows_grad,
    rows_out,
    send_mix,
    recv_mix,
    send_back,
    recv_back,
    partial,
    recv_line,
    send_group,
    recv_group,
    send_depth,
    recv_depth,
    send_last,
    recv_last,
    load_sems,
    mix_sems,
    back_sems,
    line_sems,
    group_sems,
    depth_sems,
    last_sems,
):
    me = lax.axis_index("shard")
    group = lax.axis_index("group")
    core = lax.rem(me, 2)
    across = me // 16
    deep = lax.rem(me // 2, DEPTH)
    line = across * 2 + core

    loads = [
        pltpu.make_async_copy(act_hbm, act, load_sems.at[0]),
        pltpu.make_async_copy(table_hbm, table, load_sems.at[1]),
        pltpu.make_async_copy(out_grad_hbm, out_grad, load_sems.at[2]),
    ]
    for load in loads:
        load.start()

    barrier = pltpu.get_barrier_semaphore()

    def beside(step):
        return lax.rem(me + 16 * step, SHARDS)

    @pl.loop(1, SHARDS)
    def _(step):
        peer = lax.rem(me + step, SHARDS)
        pl.semaphore_signal(barrier, inc=1, device_id=(group, peer), device_id_type=MESH)

    for step in range(1, GROUPS):
        other = lax.rem(group + step, GROUPS)
        pl.semaphore_signal(barrier, inc=1, device_id=(other, me), device_id_type=MESH)

    bias[...] = session_bias(counts, offsets)
    template = lax.broadcasted_iota(jnp.int32, (TEMPLATES, SLOTS), 0)
    hit = jnp.where(template == layout[...], 1.0, 0.0)
    chosen[...] = jnp.transpose(hit).astype(BF16)

    def remote(source, target, sems, at, peer):
        return pltpu.make_async_remote_copy(
            src_ref=source,
            dst_ref=target,
            send_sem=sems.at[(0, *at)],
            recv_sem=sems.at[(1, *at)],
            device_id=peer,
            device_id_type=MESH,
        )

    def spread(source, target, sems, pair):
        @pl.loop(1, SHARDS)
        def _(step):
            peer = lax.rem(me + SHARDS - step, SHARDS)
            remote(
                source.at[pair, peer], target.at[pair, me], sems, (pair,), (group, peer)
            ).start()

        target[pair, me] = source[pair, me]

    def several(buffer, count, sems, at):
        whole = buffer.at[pl.ds(0, count)]
        return remote(whole, whole, sems, at, (group, beside(1)))

    def spatial_step(pair):
        lanes = pl.ds(pl.multiple_of(pair * LANES, LANES), LANES)
        rows = mm(chosen[...], table[:, lanes])
        mixed = []
        for patch in range(2):
            values = (act[0, patch, :, lanes].astype(F32) + rows).astype(BF16)
            embedded[patch, pair] = values
            out, weights = spatial_pair(values, bias[...])
            for head in range(2):
                saved[patch, pair, head] = weights[head]
            mixed.append(out)
        send_mix[pair] = weave(mixed[0], mixed[1], pltpu.roll).astype(BF16)

    def temporal_step(pair):
        lanes = pl.ds(pl.multiple_of(pair * LANES, LANES), LANES)
        rows_in[...] = recv_mix[pair].astype(F32).reshape(PATCHES * 4, LANES)
        rows_grad[:, 0:4, :] = out_grad[0, :, :, lanes].astype(F32)
        flat_grad = rows_grad.reshape(PATCHES * 8, LANES)
        for slot in range(4):
            values = rows_in[pl.ds(slot, PATCHES, stride=4), :].astype(BF16)
            cotangent = flat_grad[pl.ds(slot, PATCHES, stride=8), :].astype(BF16)
            rows_out[pl.ds(slot, PATCHES, stride=4), :] = temporal_pair(values, cotangent)
        send_back[pair] = rows_out[...].reshape(SHARDS, 8, LANES).astype(BF16)

    def back_step(pair):
        lanes = pl.ds(pl.multiple_of(pair * LANES, LANES), LANES)
        grads = unweave(recv_back[pair].astype(F32), pltpu.roll)
        electrode = None
        for patch in range(2):
            full = spatial_back_pair(
                embedded[patch, pair],
                [saved[patch, pair, head] for head in range(2)],
                grads[patch].astype(BF16),
            )
            input_grad[0, patch, :, lanes] = full.astype(BF16)
            electrode = full if electrode is None else electrode + full
        turned = jnp.transpose(electrode).astype(BF16)
        partial[pair] = turned.reshape(LANES // SLICE, SLICE, SLOTS)

    def on_line(step):
        other = lax.rem(line + step, LINE)
        return other, (group, (other // 2) * 16 + deep * 2 + lax.rem(other, 2))

    def send_line(duo):
        for step in range(1, LINE):
            other, peer = on_line(step)
            block = partial.at[2 * duo + lax.rem(other, 2), other // 2]
            remote(block, recv_line.at[duo, line], line_sems, (duo,), peer).start()
        recv_line[duo, line] = partial[2 * duo + core, across]

    def group_copies(stage):
        first, count = STAGES[stage]
        span = pl.ds(first, count)
        copies = []
        for step in range(1, GROUPS):
            other = lax.rem(group + step, GROUPS)
            source, target = send_group.at[other, span], recv_group.at[step, span]
            copies.append(remote(source, target, group_sems, (stage, step), (other, me)))
        return copies

    def sum_line(stage):
        first, count = STAGES[stage]
        highs, lows = [], []
        for duo in range(first, first + count):
            several(recv_line.at[duo], LINE - 1, line_sems, (duo,)).wait_recv()
            columns = jnp.sum(recv_line[duo].astype(F32), axis=0)
            high = columns.astype(BF16)
            highs.append(high)
            lows.append((columns - high.astype(F32)).astype(BF16))
        both = mm(jnp.concatenate(highs + lows, axis=0), chosen[...])
        own = (both[: count * SLICE] + both[count * SLICE :]).astype(BF16)
        for other in range(GROUPS):
            rows = own[:, other * OWN_ROWS : (other + 1) * OWN_ROWS]
            send_group[other, first : first + count] = rows.reshape(count, SLICE, OWN_ROWS)
        for copy in group_copies(stage):
            copy.start()

    def sum_groups(stage):
        first, count = STAGES[stage]
        span = pl.ds(first, count)
        part = send_group[group, span].astype(F32)
        for step, copy in enumerate(group_copies(stage)):
            copy.wait_recv()
            part = part + recv_group[step + 1, span].astype(F32)
        send_depth[span] = part.astype(BF16)
        for step in range(1, DEPTH):
            peer = (group, across * 16 + lax.rem(deep + step, DEPTH) * 2 + core)
            target = recv_depth.at[deep, span]
            remote(send_depth.at[span], target, depth_sems, (stage,), peer).start()
        recv_depth[deep, span] = part.astype(BF16)

    def wide(buffer, stage):
        first, count = STAGES[stage]
        return buffer.at[:, pl.ds(first, count)]

    def sum_depth(stage):
        first, count = STAGES[stage]
        span = pl.ds(first, count)
        several(wide(recv_depth, stage), DEPTH - 1, depth_sems, (stage,)).wait_recv()
        total = recv_depth[0, span].astype(F32)
        for other in range(1, DEPTH):
            total = total + recv_depth[other, span].astype(F32)
        send_last[span] = total.astype(BF16)
        for step in range(1, LINE):
            _, peer = on_line(step)
            target = recv_last.at[line, span]
            remote(send_last.at[span], target, last_sems, (stage,), peer).start()
        recv_last[line, span] = total.astype(BF16)

    def write_table(stage):
        first, count = STAGES[stage]
        several(wide(recv_last, stage), LINE - 1, last_sems, (stage,)).wait_recv()
        for duo in range(first, first + count):
            for side in range(2):
                parts = [recv_last[2 * k + side, duo] for k in range(LANES // SLICE)]
                turned = jnp.transpose(jnp.concatenate(parts, axis=0).astype(F32))
                start = (2 * duo + side) * LANES
                table_grad[:, start : start + LANES] = turned

    loads[0].wait()
    loads[1].wait()

    spatial_step(0)
    pl.semaphore_wait(barrier, SHARDS - 1 + GROUPS - 1)
    spread(send_mix, recv_mix, mix_sems, 0)

    @pl.loop(1, PAIRS)
    def _(pair):
        spatial_step(pair)
        spread(send_mix, recv_mix, mix_sems, pair)

    loads[2].wait()

    @pl.loop(0, PAIRS)
    def _(pair):
        several(recv_mix.at[pair], SHARDS - 1, mix_sems, (pair,)).wait_recv()
        temporal_step(pair)
        spread(send_back, recv_back, back_sems, pair)

    @pl.loop(0, PAIRS)
    def _(pair):
        several(recv_back.at[pair], SHARDS - 1, back_sems, (pair,)).wait_recv()
        back_step(pair)

        @pl.when(lax.rem(pair, 2) == 1)
        def _():
            send_line(pair // 2)

    sum_line(0)
    sum_line(1)
    sum_groups(0)
    sum_groups(1)
    sum_depth(0)
    sum_depth(1)
    write_table(0)
    write_table(1)

    @pl.loop(0, PAIRS)
    def _(pair):
        several(send_mix.at[pair], SHARDS - 1, mix_sems, (pair,)).wait_send()
        several(send_back.at[pair], SHARDS - 1, back_sems, (pair,)).wait_send()

    for duo in range(DUOS):
        several(recv_line.at[duo], LINE - 1, line_sems, (duo,)).wait_send()
    for stage in range(len(STAGES)):
        several(wide(recv_depth, stage), DEPTH - 1, depth_sems, (stage,)).wait_send()
        several(wide(recv_last, stage), LINE - 1, last_sems, (stage,)).wait_send()
        for copy in group_copies(stage):
            copy.wait_send()


def body(activations, out_grad, embedding, counts, offsets, layout):
    vmem = pl.BlockSpec(memory_space=pltpu.VMEM)
    smem = pl.BlockSpec(memory_space=pltpu.SMEM)
    hbm = pl.BlockSpec(memory_space=pltpu.HBM)
    blocks = pltpu.VMEM((PAIRS, SHARDS, 8, LANES), BF16)
    slices = LANES // SLICE
    rows = (DUOS, SLICE, OWN_ROWS)
    scratch = [
        pltpu.VMEM(activations.shape, BF16),
        pltpu.VMEM(out_grad.shape, BF16),
        pltpu.VMEM(embedding.shape, BF16),
        pltpu.VMEM((2, PAIRS, SLOTS, LANES), BF16),
        pltpu.VMEM((2, PAIRS, 2, SLOTS, SLOTS), BF16),
        pltpu.VMEM((SLOTS, SLOTS), F32),
        pltpu.VMEM((SLOTS, TEMPLATES), BF16),
        pltpu.VMEM((PATCHES * 4, LANES), F32),
        pltpu.VMEM((PATCHES, 8, LANES), F32),
        pltpu.VMEM((PATCHES * 4, LANES), F32),
        blocks,
        blocks,
        blocks,
        blocks,
        pltpu.VMEM((PAIRS, slices, SLICE, SLOTS), BF16),
        pltpu.VMEM((DUOS, LINE, SLICE, SLOTS), BF16),
        pltpu.VMEM((GROUPS, *rows), BF16),
        pltpu.VMEM((GROUPS, *rows), BF16),
        pltpu.VMEM(rows, BF16),
        pltpu.VMEM((DEPTH, *rows), BF16),
        pltpu.VMEM(rows, BF16),
        pltpu.VMEM((LINE, *rows), BF16),
        pltpu.SemaphoreType.DMA((3,)),
        pltpu.SemaphoreType.DMA((2, PAIRS)),
        pltpu.SemaphoreType.DMA((2, PAIRS)),
        pltpu.SemaphoreType.DMA((2, DUOS)),
        pltpu.SemaphoreType.DMA((2, len(STAGES), GROUPS)),
        pltpu.SemaphoreType.DMA((2, len(STAGES))),
        pltpu.SemaphoreType.DMA((2, len(STAGES))),
    ]
    return pl.pallas_call(
        kernel,
        out_shape=(
            pltpu.VMEM(activations.shape, BF16),
            pltpu.VMEM((OWN_ROWS, WIDTH), F32),
        ),
        in_specs=[smem, smem, hbm, hbm, hbm, vmem],
        out_specs=(vmem, vmem),
        scratch_shapes=scratch,
        compiler_params=pltpu.CompilerParams(
            collective_id=0, has_side_effects=True, vmem_limit_bytes=56 << 20
        ),
    )(counts, offsets, activations, out_grad, embedding, layout)


def solution(mesh):
    placed = (
        P("group", "shard", None, None),
        P("group", None, "shard", None),
        P(),
        P("group", None),
        P("group", None),
        P("group", None),
    )
    return jax.shard_map(
        body,
        mesh=mesh,
        in_specs=placed,
        out_specs=(P("group", "shard", None, None), P("group", None)),
        check_vma=False,
    )
```
